32 devices in a mesh: seq: 16 (over z, y, x), head: 2 (over core).
Axes of the slice: x: 2, y: 2, z: 4, core: 2. Of those that a mesh axis runs over, the one named last changes fastest.
Arguments:
- hidden_in: bfloat16 [2, 4096, 1536], P(None, 'seq'), may hold values from -6 to 6
- in_gain: bfloat16 [1536], P('seq'), may hold values from 0.5 to 1.5
- w_zx: bfloat16 [1536, 2, 3072], P('seq', None, 'head'), may hold values from -0.15625 to 0.15625
- w_bc: bfloat16 [1536, 256], P('seq'), may hold values from -0.15625 to 0.15625
- w_dt: bfloat16 [1536, 48], P('seq', 'head'), may hold values from -0.15625 to 0.15625
- conv_x: float32 [4, 3072], P(None, 'head'), may hold values from -3 to 3
- conv_x_bias: float32 [3072], P('head'), may hold values from -0.5 to 0.5
- conv_bc: float32 [4, 256], replicated, may hold values from -3 to 3
- conv_bc_bias: float32 [256], replicated, may hold values from -0.5 to 0.5
- dt_bias: float32 [48], P('head'), may hold values from -5 to -3
- a_log: float32 [48], P('head'), may hold values from -12 to 0
- d_skip: float32 [48], P('head'), may hold values from 0.5 to 1.5
- gate_gain: float32 [3072], P('head'), may hold values from 0.5 to 1.5
- w_out: bfloat16 [1536, 3072], P('seq', 'head'), may hold values from -0.109375 to 0.109375
- grad_out: float32 [2, 4096, 1536], P(None, 'seq'), may hold values from -6 to 6
Outputs:
- hidden_out: float32 [2, 4096, 1536], P(None, 'seq')
- grad_in: float32 [2, 4096, 1536], P(None, 'seq')
- g_in_gain: float32 [1536], P('seq')
- g_w_zx: float32 [1536, 2, 3072], P('seq', None, 'head')
- g_w_bc: float32 [1536, 256], P('seq')
- g_w_dt: float32 [1536, 48], P('seq', 'head')
- g_conv_x: float32 [4, 3072], P(None, 'head')
- g_conv_x_bias: float32 [3072], P('head')
- g_conv_bc: float32 [4, 256], replicated
- g_conv_bc_bias: float32 [256], replicated
- g_dt_bias: float32 [48], P('head')
- g_a_log: float32 [48], P('head')
- g_d_skip: float32 [48], P('head')
- g_gate_gain: float32 [3072], P('head')
- g_w_out: float32 [1536, 3072], P('seq', 'head')
The draws below stay inside these ranges and needn't reach their ends.
All inputs are finite; a program needn't handle non-finite values.
Results may differ from the reference program's by a relative error of at most 0.00055.
The reference program's roundings to bfloat16 on the way (of `normed_in`, `normed_gate`, `cot` and `d_zx`) count: a program that leaves them out, or rounds other values in their place, can miss the bound.
Values may be sent and summed in bfloat16 or wider, within the bound.
No kernel may reach another device: no remote copies, remote signals or barrier semaphores. Data moves between devices by JAX's collectives and lax.ppermute only.
A program may use at most 384 MiB of HBM per device.

```python
import math
import jax
import jax.numpy as jnp
from jax import lax

WIDTH = 1536
INNER = 3072
HEADS = 48
HEAD_DIM = 64
STATE = 128
CONV = 4
BLOCK_LEN = 256
LENGTH = 4096


def draw_a_log(key, part):
    values = jax.random.uniform(key, (HEADS,), jnp.float32, -12.0, 0.0)
    return values


def levels(rng, dims, cuts, least, high):
    level = 1.0
    for dim, blocks in cuts:
        heights = jax.random.uniform(jax.random.fold_in(jax.random.fold_in(rng, 6), dim), (blocks,), jnp.float32, least / len(cuts), high / len(cuts))
        level = level * jnp.repeat(jnp.exp(heights), dims[dim] // blocks).reshape((-1,) + (1,) * (len(dims) - 1 - dim))
    return level


def centred(stream_key, dims, scale, reach, split=(), kind=jnp.bfloat16):
    array = scale * jax.random.normal(stream_key, dims, jnp.float32)
    if split:
        array = array * levels(stream_key, dims, split, -0.22, 0.18)
    return jnp.clip(array, -reach, reach).astype(kind)


def setup_inputs(seed: int = 0) -> dict:
    splits = jax.random.split(jax.random.key(seed), 16)
    hidden_in = centred(splits[0], (2, LENGTH, WIDTH), 1.0, 6.0, ((1, 16),))
    in_gain = jnp.clip(1.0 + 0.1 * jax.random.normal(splits[1], (WIDTH,), jnp.float32), 0.5, 1.5).astype(jnp.bfloat16)
    w_zx = centred(splits[2], (WIDTH, 2, INNER), WIDTH ** -0.5, 0.15625, ((0, 16), (2, 2)))
    w_bc = centred(splits[3], (WIDTH, 2 * STATE), WIDTH ** -0.5, 0.15625, ((0, 16),))
    w_dt = centred(splits[4], (WIDTH, HEADS), WIDTH ** -0.5, 0.15625, ((0, 16), (1, 2)))
    conv_x = centred(splits[5], (CONV, INNER), 0.5, 3.0, ((1, 2),), jnp.float32)
    conv_x_bias = jnp.clip(jax.random.uniform(splits[6], (INNER,), jnp.float32, -0.5, 0.5) * levels(splits[6], (INNER,), ((0, 2),), -0.4, 0.0), -0.5, 0.5)
    conv_bc = centred(splits[7], (CONV, 2 * STATE), 0.5, 3.0, (), jnp.float32)
    conv_bc_bias = jnp.clip(jax.random.uniform(splits[8], (2 * STATE,), jnp.float32, -0.5, 0.5), -0.5, 0.5)
    dt_bias = jnp.clip(-5.0 + 2.0 * jax.random.uniform(splits[9], (HEADS,), jnp.float32) ** levels(splits[9], (HEADS,), ((0, 2),), -0.2, 0.2), -5.0, -3.0)
    a_log = draw_a_log(jax.random.fold_in(splits[15], 71), 0)
    d_skip = jnp.clip(0.5 + 1.0 * jax.random.uniform(splits[11], (HEADS,), jnp.float32) ** levels(splits[11], (HEADS,), ((0, 2),), -0.2, 0.2), 0.5, 1.5)
    gate_gain = jnp.clip(1.0 + 0.1 * jax.random.normal(splits[12], (INNER,), jnp.float32), 0.5, 1.5)
    w_out = centred(splits[13], (WIDTH, INNER), INNER ** -0.5, 0.109375, ((0, 16), (1, 2)))
    grad_out = centred(splits[14], (2, LENGTH, WIDTH), 1.0, 6.0, ((1, 16),), jnp.float32)
    return {"hidden_in": hidden_in, "in_gain": in_gain, "w_zx": w_zx, "w_bc": w_bc, "w_dt": w_dt, "conv_x": conv_x, "conv_x_bias": conv_x_bias, "conv_bc": conv_bc, "conv_bc_bias": conv_bc_bias, "dt_bias": dt_bias, "a_log": a_log, "d_skip": d_skip, "gate_gain": gate_gain, "w_out": w_out, "grad_out": grad_out}


EPS = 1e-05
HIGH = lax.Precision.HIGHEST

def ssd_scan(values, b_matrix, c_matrix, step_sizes, decay_log, start_state, block_len):
    total_rows = values.shape[0]
    block_count = total_rows // block_len
    position = jnp.arange(block_len)
    causal = (position[:, None] >= position[None, :]).astype(jnp.float32)

    def advance(carried, pieces):
        block_x, block_b, block_c, block_dt, block_a = pieces
        cumulative = jnp.cumsum(block_a, axis=0)
        scores = jnp.dot(block_c, block_b.T, precision=HIGH)
        spread = cumulative.T[:, :, None] - cumulative.T[:, None, :]
        weights = jnp.exp(spread * causal[None]) * causal[None] * scores[None] * block_dt.T[:, None, :]
        inside = jnp.einsum('hts,shp->thp', weights, block_x, precision=HIGH)
        across = jnp.einsum('tn,hpn->thp', block_c, carried, precision=HIGH) * jnp.exp(cumulative)[:, :, None]
        tail_weight = jnp.exp(cumulative[-1][None, :] - cumulative) * block_dt
        final_state = jnp.exp(cumulative[-1])[:, None, None] * carried + jnp.einsum('sh,shp,sn->hpn', tail_weight, block_x, block_b, precision=HIGH)
        return (final_state, inside + across)

    def blocks(stacked):
        return stacked.reshape((block_count, block_len) + stacked.shape[1:])
    final_state, outputs = lax.scan(advance, start_state, (blocks(values), blocks(b_matrix), blocks(c_matrix), blocks(step_sizes), blocks(decay_log)))
    return (outputs.reshape(values.shape), final_state)

def mixer(gate_raw, x_inner, bc_part, dt_raw, tail_rows, state, conv_x, conv_x_bias, conv_bc, conv_bc_bias, dt_bias, a_log, d_skip, gate_gain):
    before_conv = jnp.concatenate([x_inner, bc_part], axis=1)
    padded = jnp.concatenate([tail_rows, before_conv], axis=0)
    kernel = jnp.concatenate([conv_x, conv_bc], axis=1)
    convolved = jnp.concatenate([conv_x_bias, conv_bc_bias])[None, :]
    row_count = before_conv.shape[0]
    for shift_at in range(CONV):
        convolved = convolved + kernel[shift_at][None, :] * padded[shift_at:shift_at + row_count]
    active = jax.nn.silu(convolved)
    values = active[:, :INNER].reshape(row_count, HEADS, HEAD_DIM)
    b_matrix = active[:, INNER:INNER + STATE]
    c_matrix = active[:, INNER + STATE:]
    step_sizes = jax.nn.softplus(dt_raw + dt_bias)
    decay_log = -step_sizes * jnp.exp(a_log)
    mixed, final_state = ssd_scan(values, b_matrix, c_matrix, step_sizes, decay_log, state, BLOCK_LEN)
    mixed = (mixed + d_skip[None, :, None] * values).reshape(row_count, INNER)
    gated = mixed * jax.nn.silu(gate_raw)
    gate_inv = lax.rsqrt(lax.optimization_barrier(jnp.mean(gated * gated, axis=1)) + EPS)
    normed_gate = gated * gate_inv[:, None] * gate_gain
    return (normed_gate, final_state, before_conv[row_count - (CONV - 1):])

def add_pair(first_term, second_term):
    return first_term + second_term

def reference(hidden_in, in_gain, w_zx, w_bc, w_dt, conv_x, conv_x_bias, conv_bc, conv_bc_bias, dt_bias, a_log, d_skip, gate_gain, w_out, grad_out):
    block_rows = math.gcd(LENGTH, 4096)
    block_total = LENGTH // block_rows
    wide = w_zx.reshape(WIDTH, 2 * INNER)
    bc_wide = w_bc.astype(jnp.float32)
    dt_wide = w_dt.astype(jnp.float32)
    params = (conv_x, conv_x_bias, conv_bc, conv_bc_bias, dt_bias, a_log, d_skip, gate_gain)

    def front(rows_in):
        hidden_wide = rows_in.astype(jnp.float32)
        inv_in = lax.rsqrt(lax.optimization_barrier(jnp.mean(hidden_wide * hidden_wide, axis=1)) + EPS)
        normed_in = (hidden_wide * inv_in[:, None] * in_gain).astype(jnp.bfloat16)
        zx_out = jnp.dot(normed_in, wide, preferred_element_type=jnp.float32)
        bc_part = jnp.dot(normed_in, w_bc, preferred_element_type=jnp.float32)
        dt_raw = jnp.dot(normed_in, w_dt, preferred_element_type=jnp.float32)
        return (hidden_wide, inv_in, normed_in, zx_out[:, :INNER], zx_out[:, INNER:], bc_part, dt_raw)

    def forward_step(carried, rows_in):
        state, tail_rows = carried
        hidden_wide, inv_in, normed_in, gate_raw, x_inner, bc_part, dt_raw = front(rows_in)
        normed_gate, final_state, new_tail = mixer(gate_raw, x_inner, bc_part, dt_raw, tail_rows, state, *params)
        out_rows = hidden_wide + jnp.dot(normed_gate.astype(jnp.bfloat16), w_out.T, preferred_element_type=jnp.float32)
        return ((final_state, new_tail), (out_rows, state, tail_rows))

    def backward_step(carried, pieces):
        d_state, d_tail, sums = carried
        rows_in, cot_rows, state, tail_rows = pieces
        hidden_wide, inv_in, normed_in, gate_raw, x_inner, bc_part, dt_raw = front(rows_in)
        outputs, pull = jax.vjp(mixer, gate_raw, x_inner, bc_part, dt_raw, tail_rows, state, *params)
        gate_round = outputs[0].astype(jnp.bfloat16)
        cot = cot_rows.astype(jnp.bfloat16)
        d_gate_out = jnp.dot(cot, w_out, preferred_element_type=jnp.float32)
        grads = pull((d_gate_out, d_state, d_tail))
        d_zx = jnp.concatenate([grads[0], grads[1]], axis=1).astype(jnp.bfloat16)
        d_bc = grads[2]
        d_dt_raw = grads[3]
        d_normed = jnp.dot(d_zx, wide.T, preferred_element_type=jnp.float32)
        d_normed = d_normed + jnp.dot(d_bc, bc_wide.T, precision=HIGH) + jnp.dot(d_dt_raw, dt_wide.T, precision=HIGH)
        normed_wide = normed_in.astype(jnp.float32)
        scaled_in = d_normed * in_gain
        grad_rows = cot_rows + inv_in[:, None] * scaled_in - hidden_wide * (inv_in ** 3 * lax.optimization_barrier(jnp.mean(scaled_in * hidden_wide, axis=1)))[:, None]
        terms = (lax.optimization_barrier(jnp.sum(d_normed * hidden_wide * inv_in[:, None], axis=0)), jnp.dot(normed_in.T, d_zx, preferred_element_type=jnp.float32).reshape(WIDTH, 2, INNER), jnp.dot(normed_wide.T, d_bc, precision=HIGH), jnp.dot(normed_wide.T, d_dt_raw, precision=HIGH)) + tuple(grads[6:]) + (jnp.dot(cot.T, gate_round, preferred_element_type=jnp.float32),)
        sums = jax.tree.map(add_pair, sums, terms)
        return ((grads[5], grads[4], sums), grad_rows)
    sums = (jnp.zeros((WIDTH,), jnp.float32), jnp.zeros((WIDTH, 2, INNER), jnp.float32), jnp.zeros((WIDTH, 2 * STATE), jnp.float32), jnp.zeros((WIDTH, HEADS), jnp.float32)) + tuple((jnp.zeros(param.shape, jnp.float32) for param in params)) + (jnp.zeros((WIDTH, INNER), jnp.float32),)
    zero_state = jnp.zeros((HEADS, HEAD_DIM, STATE), jnp.float32)
    zero_tail = jnp.zeros((CONV - 1, INNER + 2 * STATE), jnp.float32)
    out_parts = []
    grad_parts = []
    for sequence in range(2):
        rows_seq = hidden_in[sequence].reshape(block_total, block_rows, WIDTH)
        cot_seq = grad_out[sequence].reshape(block_total, block_rows, WIDTH)
        _, (out_blocks, states, tails) = lax.scan(forward_step, (zero_state, zero_tail), rows_seq)
        (_, _, sums), grad_blocks = lax.scan(backward_step, (zero_state, zero_tail, sums), (rows_seq, cot_seq, states, tails), reverse=True)
        out_parts.append(out_blocks.reshape(LENGTH, WIDTH))
        grad_parts.append(grad_blocks.reshape(LENGTH, WIDTH))
    hidden_out = jnp.stack(out_parts, axis=0)
    grad_in = jnp.stack(grad_parts, axis=0)
    return (hidden_out, grad_in, sums[0], sums[1], sums[2], sums[3], sums[4], sums[5], sums[6], sums[7], sums[8], sums[9], sums[10], sums[11], sums[12])
```

```python
from functools import partial
import math

import jax
import jax.numpy as jnp
from jax import lax
from jax.experimental import pallas as pl
from jax.experimental.pallas import tpu as pltpu
from jax.sharding import PartitionSpec as P

BLOCK_LEN = 256
EPS = 1e-05
LANES = 128
FAR = -1e30
bf16, f32 = jnp.bfloat16, jnp.float32

NN = ((1,), (0,))
NT = ((1,), (1,))
TN = ((0,), (0,))


def mm(a, b, dims):
    return lax.dot_general(a, b, (dims, ((), ())), preferred_element_type=f32)


def split2(x):
    hi = x.astype(bf16)
    return hi, (x - hi.astype(f32)).astype(bf16)


def split3(x):
    hi = x.astype(bf16)
    rest = x - hi.astype(f32)
    mid = rest.astype(bf16)
    return hi, mid, (rest - mid.astype(f32)).astype(bf16)


def dot3(a, b, dims):
    return mm(a[0], b[0], dims) + (mm(a[0], b[1], dims) + mm(a[1], b[0], dims))


def dot_exact(a, ones, dims):
    hi, mid, lo = split3(a)
    return mm(hi, ones, dims) + (mm(mid, ones, dims) + mm(lo, ones, dims))


def dot_ones(ones, a, dims):
    hi, mid, lo = split3(a)
    return mm(ones, hi, dims) + (mm(ones, mid, dims) + mm(ones, lo, dims))


def widen(v, heads, head_dim):
    rows = v.shape[0]
    per = LANES // head_dim
    lane = lax.broadcasted_iota(jnp.int32, (rows, LANES), 1)
    parts = []
    for first in range(0, heads, per):
        part = jnp.broadcast_to(v[:, first : first + 1], (rows, LANES))
        for i in range(1, per):
            other = jnp.broadcast_to(v[:, first + i : first + i + 1], (rows, LANES))
            part = jnp.where(lane < i * head_dim, part, other)
        parts.append(part)
    return jnp.concatenate(parts, axis=1)


def softplus(x):
    y = jnp.exp(-jnp.abs(x))
    z = y / (2.0 + y)
    s = z * z
    poly = 1.0 / 19
    for n in (17, 15, 13, 11, 9, 7, 5, 3, 1):
        poly = poly * s + 1.0 / n
    return jnp.maximum(x, 0.0) + 2.0 * z * poly


def sigmoid(x):
    return 1.0 / (1.0 + jnp.exp(-x))


def lower_ones(n):
    row = lax.broadcasted_iota(jnp.int32, (n, n), 0)
    col = lax.broadcasted_iota(jnp.int32, (n, n), 1)
    return (row >= col).astype(f32).astype(bf16)


def head_sum_matrix(chan, head_dim):
    row = lax.broadcasted_iota(jnp.int32, (chan, LANES), 0)
    col = lax.broadcasted_iota(jnp.int32, (chan, LANES), 1)
    return ((row // head_dim) == col).astype(f32).astype(bf16)


def conv_state_kernel(dims, proj, halo, taps, rows, act, cv, dc, lst, pw, fin, pad, state, weight):
    heads, head_dim, chan, state_dim, tap_count, nb = dims
    j = pl.program_id(1)
    q = proj.shape[0]
    mix = chan + 2 * state_dim

    @pl.when(j == 0)
    def _():
        pad[0:8] = halo[0]
        state[...] = jnp.zeros_like(state)
        weight[...] = jnp.ones_like(weight)

    pad[8 : 8 + q] = proj[:, :mix]
    conv = taps[tap_count : tap_count + 1]
    for k in range(tap_count):
        conv = conv + taps[k : k + 1] * pad[9 - tap_count + k : 9 - tap_count + k + q]
    pad[0:8] = pad[q : q + 8]
    active = conv * sigmoid(conv)
    cv[...] = conv
    act[...] = active
    steps = softplus(proj[:, mix:] + rows[0:1])
    decay = -steps * rows[1:2]
    cum = dot_ones(lower_ones(q), decay, NN)
    dc[:, :LANES] = steps
    dc[:, LANES:] = cum
    total = cum[q - 1 : q]
    u_tail = active[:, :chan] * widen(steps * jnp.exp(total - cum), heads, head_dim)
    new = dot3(split2(active[:, chan : chan + state_dim]), split2(u_tail), TN)
    lst[0] = state[...]
    pw[0] = weight[...]
    keep = widen(jnp.broadcast_to(jnp.exp(total), (8, LANES)), heads, head_dim)
    state[...] = state[...] * keep[0:1] + new
    weight[...] = weight[...] * keep

    @pl.when(j == nb - 1)
    def _():
        fin[0, :state_dim] = state[...]
        fin[0, state_dim:] = weight[...]


def inside_kernel(dims, act, dc, rows, out):
    heads, head_dim, chan, state_dim = dims
    q = act.shape[0]
    x = act[:, :chan]
    cum = dc[:, LANES:]
    cum_row = jnp.transpose(cum)
    scores = dot3(split2(act[:, chan + state_dim :]), split2(act[:, chan : chan + state_dim]), NT)
    u = x * widen(dc[:, :LANES], heads, head_dim)
    u_hi, u_lo = split2(u)
    later = lax.broadcasted_iota(jnp.int32, (q, q), 0) >= lax.broadcasted_iota(jnp.int32, (q, q), 1)
    parts = []
    for h in range(heads):
        at = slice(h * head_dim, (h + 1) * head_dim)
        gap = cum[:, h : h + 1] - cum_row[h : h + 1]
        weights = jnp.exp(jnp.where(later, gap, FAR)) * scores
        parts.append(dot3(split2(weights), (u_hi[:, at], u_lo[:, at]), NN))
    skip = widen(jnp.broadcast_to(rows[2:3], (8, LANES)), heads, head_dim)[0:1]
    out[...] = jnp.concatenate(parts, axis=1) + skip * x


def gate_kernel(dims, cm, dc, lst, pw, came, inside, gate, dgo, gain, mixed, sums):
    heads, head_dim, chan, state_dim = dims
    q = cm.shape[0]
    states = lst[0] + pw[0][0:1] * came[0][:state_dim]
    reach = widen(jnp.exp(dc[...]), heads, head_dim)
    mix = inside[...] + dot3(split2(cm[...]), split2(states), NN) * reach
    mixed[...] = mix
    g = gate[...]
    gated = mix * (g * sigmoid(g))
    scaled = dgo[...] * gain[0:1]
    lane = lax.broadcasted_iota(jnp.int32, (q, LANES), 1)
    one = jnp.sum(gated * gated, axis=1, keepdims=True)
    two = jnp.sum(scaled * gated, axis=1, keepdims=True)
    sums[0] = jnp.transpose(jnp.where(lane == 0, one, two))[:8]


def gate_back_kernel(
    dims, mixed, gate, dgo, sums, act, dc, gain, rows, ng, dgate, dmix, ldst, dw, dots, ggain, dfin, grad, weight
):
    heads, head_dim, chan, state_dim, nb, inner_all = dims
    b, j = pl.program_id(0), pl.program_id(1)
    q = mixed.shape[0]

    @pl.when((b == 0) & (j == 0))
    def _():
        ggain[...] = jnp.zeros_like(ggain)

    @pl.when(j == 0)
    def _():
        grad[...] = jnp.zeros_like(grad)
        weight[...] = jnp.ones_like(weight)

    both = jnp.transpose(jnp.concatenate([sums[0], jnp.zeros((LANES - 8, q), f32)], axis=0))
    inv = lax.rsqrt(both[:, 0:1] / inner_all + EPS)
    mix = mixed[...]
    g = gate[...]
    sig = sigmoid(g)
    gate_act = g * sig
    gated = mix * gate_act
    d_out = dgo[...]
    unit = gated * inv
    ng[...] = (unit * gain[0:1]).astype(bf16)
    scaled = d_out * gain[0:1]
    d_gated = inv * scaled - gated * (inv * inv * inv * both[:, 1:2] / inner_all)
    d_mix = d_gated * gate_act
    dmix[...] = d_mix
    dgate[...] = (d_gated * mix * sig * (1.0 + g * (1.0 - sig))).astype(bf16)
    x = act[:, :chan]
    ggain[0:1] += jnp.sum(d_out * unit, axis=0, keepdims=True)
    ggain[1:2] += jnp.sum(d_mix * x, axis=0, keepdims=True)
    skip = widen(jnp.broadcast_to(rows[2:3], (8, LANES)), heads, head_dim)[0:1]
    dots[...] = dot_exact(d_mix * (mix - skip * x), head_sum_matrix(chan, head_dim), NN)
    cum = dc[:, LANES:]
    d_reach = d_mix * widen(jnp.exp(cum), heads, head_dim)
    new = dot3(split2(act[:, chan + state_dim :]), split2(d_reach), TN)
    ldst[0] = grad[...]
    dw[0] = weight[...]
    keep = widen(jnp.broadcast_to(jnp.exp(cum[q - 1 : q]), (8, LANES)), heads, head_dim)
    grad[...] = grad[...] * keep[0:1] + new
    weight[...] = weight[...] * keep

    @pl.when(j == nb - 1)
    def _():
        dfin[0, :state_dim] = grad[...]
        dfin[0, state_dim:] = weight[...]


def inside_back_kernel(dims, act, dc, dmix, du, dbc):
    heads, head_dim, chan, state_dim = dims
    q = act.shape[0]
    cum = dc[:, LANES:]
    cum_row = jnp.transpose(cum)
    b_mat = split2(act[:, chan : chan + state_dim])
    c_mat = split2(act[:, chan + state_dim :])
    scores = dot3(b_mat, c_mat, NT)
    u_hi, u_lo = split2(act[:, :chan] * widen(dc[:, :LANES], heads, head_dim))
    y_hi, y_lo = split2(dmix[...])
    later = lax.broadcasted_iota(jnp.int32, (q, q), 1) >= lax.broadcasted_iota(jnp.int32, (q, q), 0)
    d_scores = jnp.zeros((q, q), f32)
    parts = []
    for h in range(heads):
        at = slice(h * head_dim, (h + 1) * head_dim)
        gap = cum_row[h : h + 1] - cum[:, h : h + 1]
        mixing = jnp.exp(jnp.where(later, gap, FAR))
        y = (y_hi[:, at], y_lo[:, at])
        d_scores = d_scores + mixing * dot3((u_hi[:, at], u_lo[:, at]), y, NT)
        parts.append(dot3(split2(mixing * scores), y, NN))
    du[...] = jnp.concatenate(parts, axis=1)
    d_scores = split2(d_scores)
    dbc[:, :state_dim] = dot3(d_scores, c_mat, NN)
    dbc[:, state_dim:] = dot3(d_scores, b_mat, TN)


def state_back_kernel(
    dims, act, cv, dtr, dc, dmix, du_in, dbc_in, dots, lst, pw, lst2, pw2, fin, came, ldst, dw, dcame, rows,
    dconv, ddt, gsmall, gbias
):
    heads, head_dim, chan, state_dim, nb = dims
    b, j = pl.program_id(0), pl.program_id(1)
    q = act.shape[0]

    @pl.when((b == 0) & (j == 0))
    def _():
        gsmall[...] = jnp.zeros_like(gsmall)
        gbias[...] = jnp.zeros_like(gbias)

    x = act[:, :chan]
    steps = dc[:, :LANES]
    cum = dc[:, LANES:]
    total = cum[q - 1 : q]
    before = lst[0] + pw[0][0:1] * came[0][:state_dim]
    last = j == nb - 1
    behind = jnp.where(last, fin[0][:state_dim], lst2[0])
    behind = behind + jnp.where(last, fin[0][state_dim : state_dim + 1], pw2[0][0:1]) * came[0][:state_dim]
    d_state = ldst[0] + dw[0][0:1] * dcame[0][:state_dim]
    steps_wide = widen(steps, heads, head_dim)
    tail_wide = widen(jnp.exp(total - cum), heads, head_dim)
    reach_wide = widen(jnp.exp(cum), heads, head_dim)
    d_state2 = split2(d_state)
    d_mix = dmix[...]
    d_u = du_in[...] + dot3(split2(act[:, chan : chan + state_dim]), d_state2, NN) * tail_wide
    d_b = dbc_in[:, :state_dim] + dot3(split2(x * steps_wide * tail_wide), d_state2, NT)
    d_c = dbc_in[:, state_dim:] + dot3(split2(d_mix * reach_wide), split2(before), NT)
    to_heads = head_sum_matrix(chan, head_dim)
    dot_u = dot_exact(d_u * x, to_heads, NN)
    d_cum = dots[...] - steps * dot_u
    d_total = jnp.broadcast_to(jnp.sum(d_state * behind, axis=0, keepdims=True), (8, chan))
    d_total = dot_exact(d_total, to_heads, NN)[0:1]
    d_decay = dot_ones(lower_ones(q), d_cum, TN) + d_total
    d_steps = dot_u - d_decay * rows[1:2]
    d_dt = d_steps * sigmoid(dtr[...] + rows[0:1])
    ddt[...] = d_dt
    gsmall[0:1] += jnp.sum(d_dt, axis=0, keepdims=True)
    gsmall[1:2] += jnp.sum(d_decay * (-steps * rows[1:2]), axis=0, keepdims=True)
    skip = widen(jnp.broadcast_to(rows[2:3], (8, LANES)), heads, head_dim)[0:1]
    d_x = d_u * steps_wide + skip * d_mix

    def through(lo, hi, d_active):
        conv = cv[:, lo:hi]
        sig = sigmoid(conv)
        d_conv = d_active * sig * (1.0 + conv * (1.0 - sig))
        dconv[:, lo:hi] = d_conv
        gbias[0:1, lo:hi] += jnp.sum(d_conv, axis=0, keepdims=True)

    through(0, chan, d_x)
    through(chan, chan + state_dim, d_b)
    through(chan + state_dim, chan + 2 * state_dim, d_c)


def conv_back_kernel(dims, dconv, following, dnext, proj, ddt, taps, dinner, dbc, gtaps, pad):
    chan, mix, tap_count, nb = dims
    b, j = pl.program_id(0), pl.program_id(1)
    q = dconv.shape[0]

    @pl.when((b == 0) & (j == 0))
    def _():
        gtaps[...] = jnp.zeros_like(gtaps)

    pad[:q] = dconv[...]
    pad[q:] = jnp.where(j == nb - 1, dnext[0], following[...])
    before = proj[:, :mix]
    total = jnp.zeros((q, mix), f32)
    for k in range(tap_count):
        moved = pad[tap_count - 1 - k : tap_count - 1 - k + q]
        total = total + taps[k : k + 1] * moved
        gtaps[k : k + 1] += jnp.sum(before * moved, axis=0, keepdims=True)
    dinner[:, :chan] = total[:, :chan].astype(bf16)
    d_dt = ddt[...]
    hi = d_dt.astype(bf16).astype(f32)
    lo = (d_dt - hi).astype(bf16).astype(f32)
    dinner[:, chan:] = (hi + pltpu.roll(lo, LANES // 2, 1)).astype(bf16)
    dbc[...] = total[:, chan:]


def place(pieces, slots, shape, lead=0):
    count, depth = len(pieces), slots.shape[1]

    def kernel(slot, *refs):
        out, held, came, gone = refs[count : count + 4]
        places = [(slice(None),) * lead + tuple(slot[i, n] for n in range(depth)) for i in range(count)]
        reads = [pltpu.make_async_copy(refs[i], held.at[places[i]], came.at[i]) for i in range(count)]
        writes = [pltpu.make_async_copy(held.at[places[i]], out.at[places[i]], gone.at[i]) for i in range(count)]
        for read in reads:
            read.start()
        for read, write in zip(reads, writes):
            read.wait()
            write.start()
        for write in writes:
            write.wait()

    return pl.pallas_call(
        kernel,
        out_shape=jax.ShapeDtypeStruct(shape, pieces[0].dtype),
        grid_spec=pltpu.PrefetchScalarGridSpec(
            num_scalar_prefetch=1,
            grid=(1,),
            in_specs=[pl.BlockSpec(memory_space=pl.ANY)] * count,
            out_specs=pl.BlockSpec(memory_space=pl.ANY),
            scratch_shapes=[
                pltpu.VMEM(shape, pieces[0].dtype),
                pltpu.SemaphoreType.DMA((count,)),
                pltpu.SemaphoreType.DMA((count,)),
            ],
        ),
        cost_estimate=pl.CostEstimate(
            flops=0, transcendentals=0, bytes_accessed=2 * math.prod(shape) * pieces[0].dtype.itemsize
        ),
        name="place",
    )(slots.astype(jnp.int32), *pieces)


def call(kernel, name, grid, ins, outs, scratch=(), scalars=(), flops=0):
    moved = sum(a.size * a.dtype.itemsize for a, _, _ in ins)
    moved += sum(math.prod(s) * jnp.dtype(d).itemsize for s, d, _, _ in outs)
    return pl.pallas_call(
        kernel,
        out_shape=[jax.ShapeDtypeStruct(s, d) for s, d, _, _ in outs],
        grid_spec=pltpu.PrefetchScalarGridSpec(
            num_scalar_prefetch=len(scalars),
            grid=grid,
            in_specs=[pl.BlockSpec(b, m) for _, b, m in ins],
            out_specs=[pl.BlockSpec(b, m) for _, _, b, m in outs],
            scratch_shapes=list(scratch),
        ),
        compiler_params=pltpu.CompilerParams(
            dimension_semantics=("arbitrary",) * len(grid), vmem_limit_bytes=56 << 20
        ),
        cost_estimate=pl.CostEstimate(flops=flops, transcendentals=0, bytes_accessed=moved),
        name=name,
    )(*scalars, *[a for a, _, _ in ins])


def project_kernel(hidden, gain, w, normed, out):
    wide = hidden[...].astype(f32)
    inv = lax.rsqrt(jnp.mean(wide * wide, axis=1, keepdims=True) + EPS)
    n = (wide * inv * gain[0:1].astype(f32)).astype(bf16)
    normed[...] = n
    out[...] = mm(n, w[...], NN)


def back_kernel(count, group, half, place_of, *refs):
    pairs, refs = refs[: 2 * count], refs[2 * count :]
    total = None
    for i in range(count):
        lhs, rhs = pairs[2 * i], pairs[2 * i + 1]
        part = mm(lhs[...], rhs[...], NT)
        total = part if total is None else total + part
    k = pl.program_id(0)
    for i in range(group):
        @pl.when(k == i)
        def _():
            refs[i][0] = total


def d_normed_kernel(group, chan, scalars, dg, dg2, di, di2, bc, bc2, hidden, wz, wz2, wx, wx2, dtw, dtw2, bcw, *refs):
    outs, ggain = refs[:group], refs[group]
    k, b = pl.program_id(0), pl.program_id(1)
    hi, lo = split2(bc[...] + bc2[...])
    total = mm(dg[...], wz[...], NT) + mm(dg2[...], wz2[...], NT)
    total = total + mm(di[:, :chan], wx[...], NT) + mm(di2[:, :chan], wx2[...], NT)
    total = total + mm(di[:, chan:], dtw[...], NN) + mm(di2[:, chan:], dtw2[...], NN)
    total = total + (mm(hi, bcw[...], NT) + mm(lo, bcw[...], NT))
    for i in range(group):
        @pl.when(k == i)
        def _():
            outs[i][0] = total
    wide = hidden[...].astype(f32)
    inv = lax.rsqrt(jnp.mean(wide * wide, axis=1, keepdims=True) + EPS)
    half = total.shape[1]
    mine = jnp.where(scalars[1] == 0, wide[:, :half], wide[:, half:])

    @pl.when((k == 0) & (b == 0))
    def _():
        ggain[...] = jnp.zeros_like(ggain)

    ggain[0:1] += jnp.sum(total * (mine * inv), axis=0, keepdims=True)


def gate_grad_kernel(blocks, scalars, normed, cot, dg, ng, *outs):
    k = pl.program_id(0)
    chan = dg.shape[1]
    left = mm(normed[...], dg[...], TN)
    right = mm(cot[...], ng[...], TN)
    for i in range(blocks):
        @pl.when(k == i)
        def _():
            outs[i][:, :chan] = left
            outs[i][:, chan:] = right


def inner_grad_kernel(blocks, chan, scalars, normed, di, bc, bc2, *refs):
    outs, gdt = refs[:blocks], refs[blocks]
    k = pl.program_id(0)
    n = normed[...]
    left = mm(n, di[:, :chan], TN)
    hi, lo = split2(bc[...] + bc2[...])
    right = mm(n, hi, TN) + mm(n, lo, TN)
    gdt[...] = mm(di[:, chan:], n, TN)
    for i in range(blocks):
        @pl.when(k == i)
        def _():
            outs[i][:, :chan] = left
            outs[i][:, chan:] = right


def on_device(
    hidden_in,
    in_gain,
    w_zx,
    w_bc,
    w_dt,
    conv_x,
    conv_x_bias,
    conv_bc,
    conv_bc_bias,
    dt_bias,
    a_log,
    d_skip,
    gate_gain,
    w_out,
    grad_out,
):
    seq_size = lax.axis_size("seq")
    core_count = lax.axis_size("head")
    heads_local = w_dt.shape[1]
    group = math.gcd(math.gcd(seq_size, heads_local), 4)
    blocks = seq_size // group
    position = lax.axis_index("seq")
    blk, grp = position // group, position % group
    core = lax.axis_index("head")
    other_core = core_count - 1 - core

    seqs, rows, width = hidden_in.shape
    shard = w_zx.shape[0]
    inner_local = w_zx.shape[2]
    inner_all = inner_local * core_count
    chan = inner_local // group
    heads = heads_local // group
    head_dim = chan // heads
    state_dim = w_bc.shape[1] // 2
    taps = conv_x.shape[0]
    mix = chan + 2 * state_dim
    length = group * rows
    tokens = seqs * length
    half = width // core_count
    q = min(BLOCK_LEN, length)
    nb = length // q
    steps = seqs * nb
    part = rows // core_count
    halo_rows = 8

    def plane(x, k):
        return lax.ppermute(x, "seq", [(i, i ^ k) for i in range(seq_size)])

    def facing(x, k):
        return lax.ppermute(x, "seq", [(i, i ^ (k * group)) for i in range(seq_size)])

    def along(x, d):
        route = [(i, i + d * group) for i in range(seq_size) if 0 <= i + d * group < seq_size]
        return lax.ppermute(x, "seq", route)

    def twin(x):
        return lax.ppermute(x, "head", [(i, core_count - 1 - i) for i in range(core_count)])

    def pick(x, index, axis, size=None):
        size = x.shape[axis] // group if size is None else size
        return lax.dynamic_slice_in_dim(x, index * size, size, axis)

    def after(x, *first):
        return lax.optimization_barrier((x,) + first)[0]

    def ordered(pieces, index):
        n, bit = len(pieces), 1
        while bit < n:
            flip = (index & bit) != 0
            pieces = [jnp.where(flip, pieces[i ^ bit], pieces[i]) for i in range(n)]
            bit *= 2
        return pieces

    def lane_pair(mine, other):
        return [jnp.where(core == 0, mine, other), jnp.where(core == 0, other, mine)]

    def join_halves(x):
        return jnp.concatenate(lane_pair(x, twin(x)), axis=-1)

    def swap_in_group(pieces):
        return [pieces[0]] + [plane(pieces[k], k) for k in range(1, group)]

    def gather_blocks(x):
        pieces = [x] + [facing(x, k) for k in range(1, blocks)]
        slots = jnp.stack([blk ^ k for k in range(blocks)])[:, None]
        return place(pieces, slots, (blocks,) + x.shape)

    bc_half = jnp.where(core == 0, w_bc[:, :state_dim], w_bc[:, state_dim:])
    z_cols, x_cols = w_zx[:, 0], w_zx[:, 1]

    def pack(target):
        return jnp.concatenate([pick(x_cols, target, 1), bc_half, pick(z_cols, target, 1), pick(w_out, target, 1)], axis=1)

    def pack_small(target):
        return jnp.concatenate([pick(w_dt, target, 1).T, in_gain[None]], axis=0)

    swapped = swap_in_group([pack(grp ^ k) for k in range(group)])
    small = swap_in_group([after(pack_small(grp ^ k), *swapped) for k in range(group)])
    small = jnp.stack(ordered(small, grp))
    small = [small] + [facing(small, k) for k in range(1, blocks)]
    small = jnp.stack(ordered(small, blk))
    small = jnp.transpose(small, (2, 0, 1, 3)).reshape(heads + 1, width)
    dt_w = small[:heads]
    gain8 = jnp.broadcast_to(small[heads:], (8, width))

    w_rows = jnp.stack(ordered(swapped, grp))
    w_first, w_second = w_rows[..., : chan + state_dim], w_rows[..., chan + state_dim :]

    def gather_tokens(x, *first):
        own = x.reshape(seqs, core_count, part, width)
        mine = after(lax.dynamic_index_in_dim(own, core, 1, keepdims=False), *first)
        came = [plane(mine, k) for k in range(1, group)]
        others = [twin(c) for c in came]
        slots = [(grp, 0), (grp, 1)] + [(grp ^ k, core) for k in range(1, group)]
        slots += [(grp ^ k, other_core) for k in range(1, group)]
        slots = jnp.stack([jnp.stack([jnp.asarray(i, jnp.int32) for i in s]) for s in slots])
        out = place([own[:, 0], own[:, 1]] + came + others, slots, (seqs, group, core_count, part, width), 1)
        return out.reshape(tokens, width)

    hidden = gather_tokens(hidden_in, *swapped)
    w_first = gather_blocks(w_first).reshape(width, chan + state_dim)
    w_second = gather_blocks(after(w_second, w_first)).reshape(width, 2 * chan)
    cot = gather_tokens(grad_out.astype(bf16), hidden)
    wx = w_first[:, :chan]
    bc_w = jnp.concatenate(lane_pair(w_first[:, chan:], twin(w_first[:, chan:])), axis=1)
    dt_cols = jnp.pad(dt_w.T, ((0, 0), (0, LANES - heads)))
    side_w = jnp.concatenate([wx, bc_w, dt_cols], axis=1)
    wz, wo = w_second[:, :chan], w_second[:, chan:]

    halo_hidden = hidden.reshape(seqs, length, width)[:, length - halo_rows :]
    halo_hidden = along(halo_hidden, 1).reshape(seqs * halo_rows, width)
    cols = side_w.shape[1]
    everywhere = lambda *_: (0, 0)

    def project(x, size, n):
        return call(
            project_kernel, "project", (n,),
            [(x, (size, width), lambda i: (i, 0)), (gain8, (8, width), everywhere), (side_w, (width, cols), everywhere)],
            [((size * n, width), bf16, (size, width), lambda i: (i, 0)), ((size * n, cols), f32, (size, cols), lambda i: (i, 0))],
            flops=2 * size * n * width * cols,
        )

    normed, proj = project(hidden, q, steps)
    _, halo = project(halo_hidden, seqs * halo_rows, 1)
    halo = halo[:, :mix].reshape(seqs, halo_rows, mix)

    kernel_rows = jnp.concatenate(
        [
            jnp.concatenate([pick(conv_x, grp, 1), conv_bc], axis=1),
            jnp.concatenate([pick(conv_x_bias, grp, 0), conv_bc_bias])[None],
            jnp.zeros((8 - taps - 1, mix), f32),
        ],
        axis=0,
    )
    head_rows = jnp.stack([pick(dt_bias, grp, 0), jnp.exp(pick(a_log, grp, 0)), pick(d_skip, grp, 0)])
    head_rows = jnp.pad(head_rows, ((0, 5), (0, LANES - heads)))
    gain_mine = jnp.broadcast_to(pick(gate_gain, grp, 0)[None], (8, chan))

    def tok(n, col=0):
        return (q, n), lambda b, j: (b * nb + j, col)

    def rev(n, col=0):
        return (q, n), lambda b, j: (b * nb + nb - 1 - j, col)

    def one(*shape):
        return shape, lambda b, j: (0,) * len(shape)

    def per_block(*shape, move=lambda b, j: b * nb + j):
        return (1,) + shape, lambda b, j: (move(b, j),) + (0,) * len(shape)

    def per_seq(*shape):
        return (1,) + shape, lambda b, j: (b,) + (0,) * len(shape)

    backward = lambda b, j: b * nb + nb - 1 - j
    following = lambda b, j: jnp.minimum(b * nb + j + 1, steps - 1)
    grid = (seqs, nb)
    wide_q = (tokens, mix)
    packed = state_dim + 8

    act, cv, dc, lst, pw, fin = call(
        partial(conv_state_kernel, (heads, head_dim, chan, state_dim, taps, nb)), "conv_state", grid,
        [(proj, *tok(cols)), (halo, *per_seq(halo_rows, mix)), (kernel_rows, *one(8, mix)), (head_rows, *one(8, LANES))],
        [
            (wide_q, f32, *tok(mix)),
            (wide_q, f32, *tok(mix)),
            ((tokens, 2 * LANES), f32, *tok(2 * LANES)),
            ((steps, state_dim, chan), f32, *per_block(state_dim, chan)),
            ((steps, 8, chan), f32, *per_block(8, chan)),
            ((seqs, packed, chan), f32, *per_seq(packed, chan)),
        ],
        [pltpu.VMEM((q + 8, mix), f32), pltpu.VMEM((state_dim, chan), f32), pltpu.VMEM((8, chan), f32)],
        flops=6 * tokens * state_dim * chan,
    )

    def across(own, sign):
        found = None
        d = 1
        while d < blocks:
            came = along(own, sign * d)

            def combine(later):
                keep = later[:, state_dim : state_dim + 1]
                later_state = later * (lax.broadcasted_iota(jnp.int32, (1, packed, 1), 1) < state_dim)
                return keep * came + later_state

            found = came if found is None else combine(found)
            if 2 * d < blocks:
                own = combine(own)
            d *= 2
        return jnp.zeros_like(own) if found is None else found

    came = across(fin, 1)
    inside = call(
        partial(inside_kernel, (heads, head_dim, chan, state_dim)), "inside", grid,
        [(act, *tok(mix)), (dc, *tok(2 * LANES)), (head_rows, *one(8, LANES))],
        [((tokens, chan), f32, *tok(chan))],
        flops=40 * tokens * q * chan,
    )[0]
    gate_raw = mm(normed, wz, NN)
    d_gate_out = mm(cot, wo, NN)
    c_col, cum_col = (chan + state_dim) // state_dim, 1
    mixed, sums = call(
        partial(gate_kernel, (heads, head_dim, chan, state_dim)), "gate", grid,
        [
            (act, *tok(state_dim, c_col)),
            (dc, *tok(LANES, cum_col)),
            (lst, *per_block(state_dim, chan)),
            (pw, *per_block(8, chan)),
            (came, *per_seq(packed, chan)),
            (inside, *tok(chan)),
            (gate_raw, *tok(chan)),
            (d_gate_out, *tok(chan)),
            (gain_mine, *one(8, chan)),
        ],
        [((tokens, chan), f32, *tok(chan)), ((steps, 8, q), f32, *per_block(8, q))],
        flops=6 * tokens * state_dim * chan,
    )
    sums = sums + twin(sums)
    sums = sum(swap_in_group([sums] * group))

    ng, d_gate, d_mixed, ldst, dw, dots, g_rows, dfin = call(
        partial(gate_back_kernel, (heads, head_dim, chan, state_dim, nb, inner_all)), "gate_back", grid,
        [
            (mixed, *rev(chan)),
            (gate_raw, *rev(chan)),
            (d_gate_out, *rev(chan)),
            (sums, *per_block(8, q, move=backward)),
            (act, *rev(mix)),
            (dc, *rev(2 * LANES)),
            (gain_mine, *one(8, chan)),
            (head_rows, *one(8, LANES)),
        ],
        [
            ((tokens, chan), bf16, *rev(chan)),
            ((tokens, chan), bf16, *rev(chan)),
            ((tokens, chan), f32, *rev(chan)),
            ((steps, state_dim, chan), f32, *per_block(state_dim, chan, move=backward)),
            ((steps, 8, chan), f32, *per_block(8, chan, move=backward)),
            ((tokens, LANES), f32, *rev(LANES)),
            ((8, chan), f32, *one(8, chan)),
            ((seqs, packed, chan), f32, *per_seq(packed, chan)),
        ],
        [pltpu.VMEM((state_dim, chan), f32), pltpu.VMEM((8, chan), f32)],
        flops=8 * tokens * state_dim * chan,
    )
    d_came = across(dfin, -1)
    d_u, d_bc_in = call(
        partial(inside_back_kernel, (heads, head_dim, chan, state_dim)), "inside_back", grid,
        [(act, *tok(mix)), (dc, *tok(2 * LANES)), (d_mixed, *tok(chan))],
        [((tokens, chan), f32, *tok(chan)), ((tokens, 2 * state_dim), f32, *tok(2 * state_dim))],
        flops=80 * tokens * q * chan,
    )

    place_of = jnp.stack([grp, core, blk]).astype(jnp.int32)
    shard_rows = width // blocks

    def piece_specs(count, shape, block):
        def index(i):
            def at(k, *rest):
                b = rest[0] if len(rest) == 2 else 0
                return (jnp.where(k < i, 0, jnp.where(k == i, b, shape[0] - 1)),) + (0,) * (len(shape) - 1)

            return at

        return [(shape, f32, block, index(i)) for i in range(count)]

    def grad_pieces(count, cols):
        return [((shard_rows, cols), f32, (shard_rows, cols), lambda k, s: (0, 0))] * count

    by_rows = (tokens, shard_rows), lambda k, s: (0, s[2] ^ k)
    def cut_rows(g):
        return [pick(g, blk ^ k, 0, shard_rows) for k in range(blocks)]

    if shard_rows % LANES:
        g_second = cut_rows(jnp.concatenate([mm(normed, d_gate, TN), mm(cot, ng, TN)], axis=1))
    else:
        g_second = call(
            partial(gate_grad_kernel, blocks), "gate_grad", (blocks,),
            [
                (normed, *by_rows),
                (cot, *by_rows),
                (d_gate, (tokens, chan), lambda k, s: (0, 0)),
                (ng, (tokens, chan), lambda k, s: (0, 0)),
            ],
            grad_pieces(blocks, 2 * chan),
            scalars=[place_of],
            flops=4 * tokens * width * chan,
        )

    def sum_blocks(pieces):
        mine = pieces[0]
        for k in range(1, blocks):
            mine = mine + facing(pieces[k], k)
        return mine

    w_tail = jnp.concatenate([wx, wz, wo], axis=1)
    tail_mine = pick(w_tail, core, 0, half)
    tail_other = twin(pick(w_tail, other_core, 0, half))
    ng_other = twin(ng)
    by_piece = (rows, chan), lambda k, b, s: (b * group + (s[0] ^ k), 0)

    def weight_cols(x, n):
        return (x, (half, chan), lambda k, b, s: (0, n))

    def out_kernel(scalars, *refs):
        back_kernel(2, group, half, None, *refs)

    branch = call(
        out_kernel, "out_project", (group, seqs),
        [(ng, *by_piece), weight_cols(tail_mine, 2), (ng_other, *by_piece), weight_cols(tail_other, 2)],
        piece_specs(group, (seqs, rows, half), (1, rows, half)),
        scalars=[place_of],
        flops=4 * tokens * half * chan,
    )
    branch = sum(swap_in_group(branch)).reshape(seqs * rows, half)
    own = hidden_in.astype(f32).reshape(seqs * rows, width)
    hidden_out = (own + join_halves(branch)).reshape(seqs, rows, width)
    d_gate_other = twin(d_gate)

    d_conv, d_dt, g_small, g_bias = call(
        partial(state_back_kernel, (heads, head_dim, chan, state_dim, nb)), "state_back", grid,
        [
            (act, *tok(mix)),
            (cv, *tok(mix)),
            (proj, *tok(LANES, mix // LANES)),
            (dc, *tok(2 * LANES)),
            (d_mixed, *tok(chan)),
            (d_u, *tok(chan)),
            (d_bc_in, *tok(2 * state_dim)),
            (dots, *tok(LANES)),
            (lst, *per_block(state_dim, chan)),
            (pw, *per_block(8, chan)),
            (lst, *per_block(state_dim, chan, move=following)),
            (pw, *per_block(8, chan, move=following)),
            (fin, *per_seq(packed, chan)),
            (came, *per_seq(packed, chan)),
            (ldst, *per_block(state_dim, chan)),
            (dw, *per_block(8, chan)),
            (d_came, *per_seq(packed, chan)),
            (head_rows, *one(8, LANES)),
        ],
        [
            (wide_q, f32, *tok(mix)),
            ((tokens, LANES), f32, *tok(LANES)),
            ((8, LANES), f32, *one(8, LANES)),
            ((8, mix), f32, *one(8, mix)),
        ],
        flops=18 * tokens * state_dim * chan,
    )
    d_next = along(d_conv.reshape(seqs, length, mix)[:, :halo_rows], -1)
    eighth = q // 8
    d_inner, d_bc, g_taps = call(
        partial(conv_back_kernel, (chan, mix, taps, nb)), "conv_back", grid,
        [
            (d_conv, *tok(mix)),
            (d_conv, (8, mix), lambda b, j: (following(b, j) * eighth, 0)),
            (d_next, *per_seq(halo_rows, mix)),
            (proj, *tok(cols)),
            (d_dt, *tok(LANES)),
            (kernel_rows, *one(8, mix)),
        ],
        [
            ((tokens, chan + LANES), bf16, *tok(chan + LANES)),
            ((tokens, 2 * state_dim), f32, *tok(2 * state_dim)),
            ((8, mix), f32, *one(8, mix)),
        ],
        [pltpu.VMEM((q + 8, mix), f32)],
        flops=tokens * mix * 20,
    )

    d_bc_other = twin(d_bc)
    d_inner_other = twin(d_inner)
    bc_cols = (tokens, state_dim), lambda k, s: (0, s[1])
    if shard_rows % LANES:
        bc_sum = lax.dynamic_slice_in_dim(d_bc + d_bc_other, core * state_dim, state_dim, 1)
        bc_hi = lax.reduce_precision(bc_sum, 8, 7)
        bc_terms = (bc_hi.astype(bf16), (bc_sum - bc_hi).astype(bf16))
        first = cut_rows(
            jnp.concatenate([mm(normed, d_inner[:, :chan], TN), sum(mm(normed, p, TN) for p in bc_terms)], axis=1)
        ) + [mm(d_inner[:, chan:], normed, TN)]
    else:
        first = call(
            partial(inner_grad_kernel, blocks, chan), "inner_grad", (blocks,),
            [
                (normed, *by_rows),
                (d_inner, (tokens, chan + LANES), lambda k, s: (0, 0)),
                (d_bc, *bc_cols),
                (d_bc_other, *bc_cols),
            ],
            grad_pieces(blocks, chan + state_dim) + [((LANES, width), f32, (LANES, shard_rows), lambda k, s: (0, s[2] ^ k))],
            scalars=[place_of],
            flops=2 * tokens * width * (chan + 3 * LANES),
        )
    g_first, g_dt_rows = first[:blocks], first[blocks]
    g_dt_rows = g_dt_rows[:heads] + g_dt_rows[LANES // 2 : LANES // 2 + heads]

    dtw = jnp.concatenate([jnp.pad(dt_w, ((0, LANES // 2 - heads), (0, 0)))] * 2, axis=0)
    dtw_half = pick(dtw, core, 1, half)
    dtw_other = twin(pick(dtw, other_core, 1, half))
    bcw_half = pick(bc_w, core, 0, half)
    by_piece2 = (rows, chan + LANES), by_piece[1]
    by_piece3 = (rows, 2 * state_dim), by_piece[1]
    back = call(
        partial(d_normed_kernel, group, chan), "d_normed", (group, seqs),
        [
            (d_gate, *by_piece),
            (d_gate_other, *by_piece),
            (d_inner, *by_piece2),
            (d_inner_other, *by_piece2),
            (d_bc, *by_piece3),
            (d_bc_other, *by_piece3),
            (hidden, (rows, width), by_piece[1]),
            weight_cols(tail_mine, 1),
            weight_cols(tail_other, 1),
            weight_cols(tail_mine, 0),
            weight_cols(tail_other, 0),
            (dtw_half, (LANES, half), lambda k, b, s: (0, 0)),
            (dtw_other, (LANES, half), lambda k, b, s: (0, 0)),
            (bcw_half, (half, 2 * state_dim), lambda k, b, s: (0, 0)),
        ],
        piece_specs(group, (seqs, rows, half), (1, rows, half)) + [((8, half), f32, (8, half), lambda k, b, s: (0, 0))],
        scalars=[place_of],
        flops=2 * tokens * half * (4 * chan + 6 * LANES),
    )
    d_pieces, g_gain_half = back[:group], back[group][0]
    d_normed = sum(swap_in_group(d_pieces)).reshape(seqs * rows, half)

    own_inv = lax.rsqrt(jnp.mean(own * own, axis=1) + EPS)
    scaled_in = d_normed * pick(gain8[0], core, 0, half).astype(f32)
    dot_in = jnp.sum(scaled_in * pick(own, core, 1, half), axis=1)
    dot_in = (dot_in + twin(dot_in)) / width
    grad_in = (
        grad_out.reshape(seqs * rows, width)
        + own_inv[:, None] * join_halves(scaled_in)
        - own * (own_inv**3 * dot_in)[:, None]
    ).reshape(seqs, rows, width)

    g_first = sum_blocks(g_first).reshape(group, shard, chan + state_dim)
    g_second = sum_blocks(g_second).reshape(group, shard, 2 * chan)
    both = jnp.concatenate([g_first, g_second], axis=2)
    pieces = [lax.dynamic_index_in_dim(both, grp ^ k, 0, keepdims=False) for k in range(group)]
    pieces = swap_in_group(pieces)
    g_w_bc = join_halves(sum(p[:, chan : chan + state_dim] for p in pieces))
    pieces = ordered(pieces, grp)
    lo = chan + state_dim
    g_w_x = jnp.concatenate([p[:, :chan] for p in pieces], axis=1)
    g_w_z = jnp.concatenate([p[:, lo : lo + chan] for p in pieces], axis=1)
    g_w_out = jnp.concatenate([p[:, lo + chan :] for p in pieces], axis=1)
    g_w_zx = jnp.stack([g_w_z, g_w_x], axis=1)

    g_d_skip = jnp.sum(g_rows[1].reshape(heads, head_dim), axis=1)
    conv_rows = jnp.concatenate([g_taps[:taps, chan:], g_bias[:1, chan:]], 0)
    conv_rows = conv_rows + twin(conv_rows)
    head_grads = jnp.concatenate([g_small[0, :heads], g_small[1, :heads], g_d_skip])
    spread_rows = jnp.concatenate(
        [g_taps[:taps, :chan], g_bias[:1, :chan], g_rows[:1], jnp.pad(head_grads, (0, chan - 3 * heads))[None]], 0
    )
    flat = jnp.concatenate([spread_rows.reshape(-1), conv_rows.reshape(-1), g_gain_half, g_dt_rows.reshape(-1)])
    d = 1
    while d < blocks:
        flat = flat + facing(flat, d)
        d *= 2
    n1 = spread_rows.size
    n2 = n1 + conv_rows.size
    n3 = n2 + half
    found = jnp.stack(ordered(swap_in_group([flat] * group), grp))
    spread = found[:, :n1].reshape(group, taps + 3, chan)
    wide_rows = jnp.moveaxis(spread, 0, 1).reshape(taps + 3, inner_local)
    g_conv_x, g_conv_x_bias, g_gate_gain = wide_rows[:taps], wide_rows[taps], wide_rows[taps + 1]
    head_grads = spread[:, taps + 2, : 3 * heads].reshape(group, 3, heads)
    head_grads = jnp.moveaxis(head_grads, 0, 1).reshape(3, heads_local)
    g_dt_bias, g_a_log, g_d_skip = head_grads[0], head_grads[1], head_grads[2]
    conv_sum = jnp.sum(found[:, n1:n2], axis=0).reshape(taps + 1, 2 * state_dim)
    g_conv_bc, g_conv_bc_bias = conv_sum[:taps], conv_sum[taps]
    gain_sum = join_halves(jnp.sum(found[:, n2:n3], axis=0))
    g_in_gain = lax.dynamic_slice_in_dim(gain_sum, position * shard, shard, 0)
    g_dt_all = found[:, n3:].reshape(group, heads, blocks * group, shard)
    g_w_dt = lax.dynamic_index_in_dim(g_dt_all, position, 2, keepdims=False).reshape(heads_local, shard).T

    return (
        hidden_out,
        grad_in,
        g_in_gain,
        g_w_zx,
        g_w_bc,
        g_w_dt,
        g_conv_x,
        g_conv_x_bias,
        g_conv_bc,
        g_conv_bc_bias,
        g_dt_bias,
        g_a_log,
        g_d_skip,
        g_gate_gain,
        g_w_out,
    )


def solution(mesh):
    in_specs = (
        P(None, "seq", None),
        P("seq"),
        P("seq", None, "head"),
        P("seq", None),
        P("seq", "head"),
        P(None, "head"),
        P("head"),
        P(),
        P(),
        P("head"),
        P("head"),
        P("head"),
        P("head"),
        P("seq", "head"),
        P(None, "seq", None),
    )
    out_specs = (
        P(None, "seq", None),
        P(None, "seq", None),
        P("seq"),
        P("seq", None, "head"),
        P("seq", None),
        P("seq", "head"),
        P(None, "head"),
        P("head"),
        P(),
        P(),
        P("head"),
        P("head"),
        P("head"),
        P("head"),
        P("seq", "head"),
    )
    return jax.shard_map(
        on_device, mesh=mesh, in_specs=in_specs, out_specs=out_specs, check_vma=False
    )
```
